32 devices in a mesh: seq: 16 (over z, x, core), head: 2 (over y).
Axes of the slice: x: 2, y: 2, z: 4, core: 2. Of those that a mesh axis runs over, the one named last changes fastest.
Arguments:
- queries: bfloat16 [16384, 128], P('seq'), may hold values from -0.59765625 to 0.59765625
- key_rows: bfloat16 [16384, 128], P('seq'), may hold values from -0.59765625 to 0.59765625
- value_rows: bfloat16 [16384, 4096], P('seq', 'head'), may hold values from -0.119628906 to 0.119628906
- out_grad: bfloat16 [16384, 4096], P('seq', 'head'), may hold values from -0.29882812 to 0.29882812
- level_index: int32 [16384, 5], P('seq'), may hold values from 0 to 7
- level_table: float32 [5, 8, 64], P(None, None, 'head'), may hold values from 0.25 to 2.5
Outputs:
- query_grad: bfloat16 [16384, 128], P('seq')
- key_grad: bfloat16 [16384, 128], P('seq')
- value_grad: bfloat16 [16384, 4096], P('seq', 'head')
The draws below stay inside these ranges and needn't reach their ends.
All inputs are finite; a program needn't handle non-finite values.
Results may differ from the reference program's by a relative error of at most 0.018.
Values may be sent and summed in bfloat16 or wider, within the bound.
No kernel may reach another device: no remote copies, remote signals or barrier semaphores. Data moves between devices by JAX's collectives and lax.ppermute only.
A program may use at most 128 MiB of HBM per device.

```python
import math
import jax
import jax.numpy as jnp
from jax import lax

HEADS = 64
HEAD_DIM = 64
STATE = 128
PICKS = 8
TOK_DEV = 1024
TOKENS = 16384
LEVELS = 5
N_SEQ = 16


def place_ends(entries, own_key, least, largest):
    dims = entries.shape
    spot = [jax.random.randint(jax.random.fold_in(own_key, axis), (), 0, dims[axis]) for axis in range(len(dims))]
    entries = entries.at[tuple(spot)].set(least)
    longest = dims.index(max(dims))
    spot[longest] = (spot[longest] + 1) % dims[longest]
    return entries.at[tuple(spot)].set(largest)


def steps_of(own_key, dims, split, least, top_value):
    gain = 1.0
    for axis_at, shards_of in split:
        draws = jax.random.uniform(jax.random.fold_in(jax.random.fold_in(own_key, 6), axis_at), (shards_of,), jnp.float32, least / len(split), top_value / len(split))
        gain = gain * jnp.repeat(jnp.exp(draws), dims[axis_at] // shards_of).reshape((-1,) + (1,) * (len(dims) - 1 - axis_at))
    return gain


def centred(rng, dims, scale, most, split=(), kind=jnp.bfloat16):
    gain = steps_of(rng, dims, split, -0.22, 0.18) if split else 1.0
    result = jax.random.normal(rng, dims, jnp.float32) * scale * gain
    return jnp.minimum(jnp.maximum(result, -most), most).astype(kind)


def setup_inputs(seed: int = 0) -> dict:
    arg_keys = jax.random.split(jax.random.key(seed), 7)
    queries = centred(arg_keys[0], (TOKENS, STATE), 0.1, 0.59765625, ((0, 16),))
    key_rows = centred(arg_keys[1], (TOKENS, STATE), 0.1, 0.59765625, ((0, 16),))
    value_rows = centred(arg_keys[2], (TOKENS, HEADS * HEAD_DIM), 0.02, 0.119628906, ((0, 16), (1, 2)))
    out_grad = centred(arg_keys[3], (TOKENS, HEADS * HEAD_DIM), 0.05, 0.29882812, ((0, 16), (1, 2)))
    level_index = place_ends(jax.random.randint(arg_keys[4], (TOKENS, LEVELS), 0, PICKS), jax.random.fold_in(arg_keys[4], 1), 0, PICKS - 1).astype(jnp.int32)
    level_table = jnp.clip(jnp.exp(math.log(2.5) - 2.3025851 * jax.random.uniform(arg_keys[5], (LEVELS, PICKS, HEADS), jnp.float32) ** steps_of(arg_keys[5], (LEVELS, PICKS, HEADS), ((2, 2),), -0.2, 0.2)), 0.25, 2.5)
    return dict(queries=queries, key_rows=key_rows, value_rows=value_rows, out_grad=out_grad, level_index=level_index, level_table=level_table)


def scaled_grads(grad_block, weight_block):
    count = grad_block.shape[0]
    shaped = grad_block.astype(jnp.float32).reshape(count, HEADS, HEAD_DIM)
    scaled = shaped[:, None, :, :] * weight_block[:, :, :, None]
    return scaled.reshape(count, LEVELS, HEADS * HEAD_DIM).astype(jnp.bfloat16)


def block_terms(bundle):
    query_block, key_block, value_block, grad_block, weight_block = bundle
    scaled = scaled_grads(grad_block, weight_block)
    block_state = jnp.dot(key_block.T, value_block, preferred_element_type=jnp.float32).astype(jnp.bfloat16)
    level_grads = jnp.einsum("tn,tlw->lnw", query_block.astype(jnp.float32), scaled[:, 1:].astype(jnp.float32))
    return block_state, level_grads


def finish(bundle):
    query_block, key_block, value_block, grad_block, weight_block, sibling_block, state_grad = bundle
    scaled = scaled_grads(grad_block, weight_block)
    row_ids = lax.broadcasted_iota(jnp.int32, (TOK_DEV, TOK_DEV), 0)
    col_ids = lax.broadcasted_iota(jnp.int32, (TOK_DEV, TOK_DEV), 1)
    causal = row_ids >= col_ids
    scores = jnp.dot(query_block, key_block.T, preferred_element_type=jnp.float32)
    masked = jnp.where(causal, scores, 0.0).astype(jnp.bfloat16)
    local_scaled = scaled[:, 0]
    score_grad = jnp.where(causal, jnp.dot(local_scaled, value_block.T, preferred_element_type=jnp.float32), 0.0).astype(jnp.bfloat16)
    state_low = state_grad.astype(jnp.bfloat16)
    value_grad = jnp.dot(masked.T, local_scaled, preferred_element_type=jnp.float32) + jnp.dot(key_block, state_low, preferred_element_type=jnp.float32)
    query_grad = jnp.dot(score_grad, key_block, preferred_element_type=jnp.float32) + jnp.einsum("tlw,lnw->tn", scaled[:, 1:].astype(jnp.float32), sibling_block.astype(jnp.float32))
    key_grad = jnp.dot(score_grad.T, query_block, preferred_element_type=jnp.float32) + jnp.dot(value_block, state_low.T, preferred_element_type=jnp.float32)
    return query_grad.astype(jnp.bfloat16), key_grad.astype(jnp.bfloat16), value_grad.astype(jnp.bfloat16)


def split_blocks(array):
    return array.reshape((N_SEQ, TOK_DEV) + array.shape[1:])


def reference(queries, key_rows, value_rows, out_grad, level_index, level_table):
    tree_depth = LEVELS - 1
    columns = HEADS * HEAD_DIM
    rung_ids = jnp.arange(LEVELS, dtype=jnp.int32)[None, :]
    weights = level_table[rung_ids, level_index]
    bundle = (split_blocks(queries), split_blocks(key_rows), split_blocks(value_rows), split_blocks(out_grad), split_blocks(weights))
    states, level_grads = lax.map(block_terms, bundle)
    position = jnp.arange(N_SEQ, dtype=jnp.int32)
    layered = states
    sibling_list = []
    state_grads = jnp.zeros((N_SEQ, STATE, columns), jnp.float32)
    for height in range(tree_depth):
        is_set = ((position >> height) & 1) == 1
        partner_index = (position >> height) ^ 1
        picked = jnp.take(layered, partner_index, axis=0)
        sibling_list.append(jnp.where(is_set[:, None, None], picked, jnp.zeros_like(picked)))
        layered = (layered[0::2].astype(jnp.float32) + layered[1::2].astype(jnp.float32)).astype(jnp.bfloat16)
        masked_grads = jnp.where(is_set[:, None, None], level_grads[:, height], jnp.zeros_like(level_grads[:, height]))
        summed = masked_grads.reshape((N_SEQ >> height, 1 << height, STATE, columns)).sum(axis=1)
        returned = jnp.take(summed, partner_index, axis=0)
        state_grads = state_grads + jnp.where(is_set[:, None, None], jnp.zeros_like(returned), returned)
    siblings = jnp.stack(sibling_list, axis=1)
    outputs = lax.map(finish, bundle + (siblings, state_grads))
    query_grad = outputs[0].reshape(TOKENS, STATE)
    key_grad = outputs[1].reshape(TOKENS, STATE)
    value_grad = outputs[2].reshape(TOKENS, columns)
    return query_grad, key_grad, value_grad
```

```python
import functools

import jax
import jax.numpy as jnp
from jax import lax
from jax.experimental import pallas as pl
from jax.experimental.pallas import tpu as pltpu
from jax.sharding import PartitionSpec as P

F32 = jnp.float32
BF16 = jnp.bfloat16
PARTS = 4
TILE = 256


def dot(left, right, dims=((1,), (0,))):
    return lax.dot_general(left, right, (dims, ((), ())), preferred_element_type=F32)


def exchange(block, mask):
    count = lax.axis_size("seq")
    return lax.ppermute(block, "seq", [(i, i ^ mask) for i in range(count)])


def head_sum(partial):
    count = lax.axis_size("head")
    stride = 1
    while stride < count:
        other = lax.ppermute(partial, "head", [(i, i ^ stride) for i in range(count)])
        partial = (partial.astype(F32) + other.astype(F32)).astype(BF16)
        stride *= 2
    return partial


def level_weights(index_ref, table_ref, level):
    table = table_ref[level]
    picks = table.shape[0]
    row = index_ref[level : level + 1, :]
    ids = lax.broadcasted_iota(jnp.int32, (picks, row.shape[1]), 0)
    hot = (jnp.broadcast_to(row, ids.shape) == ids).astype(F32)
    hot = jnp.concatenate([hot, hot], axis=0).astype(BF16)
    high = table.astype(BF16).astype(F32)
    terms = jnp.concatenate([high, table - high], axis=0).astype(BF16)
    return dot(terms, hot, ((0,), (0,)))


def scaled_rows(grad, weight_row, head_size, heads):
    parts = []
    for h in range(heads):
        part = grad[h * head_size : (h + 1) * head_size, :]
        weight = jnp.broadcast_to(weight_row(h), part.shape)
        parts.append((weight * part.astype(F32)).astype(BF16))
    return jnp.concatenate(parts, axis=0)


def slot_kernel(levels, head_size, make_transpose, pos_ref, *refs):
    refs = list(refs)
    q_ref, k_ref, v_ref, g_ref, index_ref, table_ref = refs[:6]
    del refs[:6]
    outs = [(refs.pop(0), refs.pop(0)) for _ in levels]
    if make_transpose:
        gt_ref = refs.pop(0)
    q_t, k_t, weights = refs
    step = pl.program_id(0)
    pos = pos_ref[0]

    @pl.when(step == 0)
    def _():
        q_t[...] = q_ref[...].T
        k_t[...] = k_ref[...].T
        for i, level in enumerate(levels):
            weights[i] = level_weights(index_ref, table_ref, level)

    if make_transpose:
        gt_ref[...] = g_ref[...].T
    else:
        gt_ref = g_ref
    width = v_ref.shape[1]
    heads = width // head_size
    first = (place_of(step) ^ (pos & 3)) * heads
    for i, (level, (send, keep)) in enumerate(zip(levels, outs)):
        bit = (pos >> (level - 1)) & 1

        def put(value):
            @pl.when(step < PARTS // 2)
            def _():
                send[0] = value

            @pl.when(step >= PARTS // 2)
            def _():
                keep[0] = value

        @pl.when(bit == 1)
        def _():
            scaled = scaled_rows(
                gt_ref[...], lambda h: weights[i, pl.ds(first + h, 1), :], head_size, heads
            )
            put(dot(q_t[...], scaled, ((1,), (1,))).astype(BF16))

        @pl.when(bit == 0)
        def _():
            put(dot(k_t[...], v_ref[...]).astype(BF16))


def place_of(step):
    half = PARTS // 2
    return jnp.where(step < half, 2 * step + 1, 2 * (step - half))


def slots(pos, q, k, v, g, index, table, levels, head_size, make_transpose):
    tokens, state = q.shape
    columns = v.shape[1]
    width = columns // PARTS
    depth, picks, heads = table.shape

    def quarter(s, p):
        return place_of(s) ^ (p[0] & 3)

    whole = lambda s, p: (0, 0)
    half = PARTS // 2
    slab = jax.ShapeDtypeStruct((half, state, width), BF16)
    out_shape = [slab] * (2 * len(levels))
    out_specs = [
        pl.BlockSpec((1, state, width), lambda s, p: (jnp.minimum(s, half - 1), 0, 0)),
        pl.BlockSpec((1, state, width), lambda s, p: (jnp.maximum(s - half, 0), 0, 0)),
    ] * len(levels)
    if make_transpose:
        g_spec = pl.BlockSpec((tokens, width), lambda s, p: (0, quarter(s, p)))
        out_shape.append(jax.ShapeDtypeStruct((columns, tokens), BF16))
        out_specs.append(pl.BlockSpec((width, tokens), lambda s, p: (quarter(s, p), 0)))
    else:
        g_spec = pl.BlockSpec((width, tokens), lambda s, p: (quarter(s, p), 0))
    return pl.pallas_call(
        functools.partial(slot_kernel, levels, head_size, make_transpose),
        grid_spec=pltpu.PrefetchScalarGridSpec(
            num_scalar_prefetch=1,
            grid=(PARTS,),
            in_specs=[
                pl.BlockSpec((tokens, state), whole),
                pl.BlockSpec((tokens, state), whole),
                pl.BlockSpec((tokens, width), lambda s, p: (0, quarter(s, p))),
                g_spec,
                pl.BlockSpec(index.shape, whole),
                pl.BlockSpec(table.shape, lambda s, p: (0, 0, 0)),
            ],
            out_specs=out_specs,
            scratch_shapes=[
                pltpu.VMEM((state, tokens), BF16),
                pltpu.VMEM((state, tokens), BF16),
                pltpu.VMEM((len(levels), heads, tokens), F32),
            ],
        ),
        out_shape=out_shape,
        cost_estimate=pl.CostEstimate(
            flops=2 * tokens * state * columns * len(levels) * 2,
            bytes_accessed=4 * tokens * columns + 4 * tokens * columns,
            transcendentals=0,
        ),
        name="slots_" + "_".join(map(str, levels)),
    )(pos, q, k, v, g, index, table)


def local_kernel(head_size, q_ref, k_ref, v_ref, gt_ref, index_ref, table_ref, qg_ref, kg_ref):
    step = pl.program_id(0)
    heads = table_ref.shape[2]
    weights = level_weights(index_ref, table_ref, 0)
    scaled = scaled_rows(gt_ref[...], lambda h: weights[h : h + 1, :], head_size, heads)
    tile = gt_ref.shape[1]
    for j in range(v_ref.shape[0] // tile):

        @pl.when(step == j)
        def _():
            rows = (j + 1) * tile
            grads = dot(v_ref[:rows, :], scaled)
            s_ids = lax.broadcasted_iota(jnp.int32, grads.shape, 0)
            t_ids = lax.broadcasted_iota(jnp.int32, grads.shape, 1) + j * tile
            grads = jnp.where(s_ids <= t_ids, grads, 0.0).astype(BF16)
            qg_ref[...] = dot(k_ref[:rows, :], grads, ((0,), (0,)))
            part = dot(grads, q_ref[...])
            if j:
                kg_ref[: rows - tile, :] += part[: rows - tile]
            kg_ref[rows - tile : rows, :] = part[rows - tile :]


def local_terms(q, k, v, gt, index, table, head_size):
    tokens, state = q.shape
    columns = v.shape[1]
    tile = min(TILE, tokens)
    whole = lambda j: (0, 0)
    return pl.pallas_call(
        functools.partial(local_kernel, head_size),
        grid=(tokens // tile,),
        in_specs=[
            pl.BlockSpec((tile, state), lambda j: (j, 0)),
            pl.BlockSpec((tokens, state), whole),
            pl.BlockSpec((tokens, columns), whole),
            pl.BlockSpec((columns, tile), lambda j: (0, j)),
            pl.BlockSpec((index.shape[0], tile), lambda j: (0, j)),
            pl.BlockSpec(table.shape, lambda j: (0, 0, 0)),
        ],
        out_specs=[
            pl.BlockSpec((state, tile), lambda j: (0, j)),
            pl.BlockSpec((tokens, state), whole),
        ],
        out_shape=[
            jax.ShapeDtypeStruct((state, tokens), F32),
            jax.ShapeDtypeStruct((tokens, state), F32),
        ],
        cost_estimate=pl.CostEstimate(
            flops=2 * tokens * tokens * columns,
            bytes_accessed=4 * tokens * columns,
            transcendentals=0,
        ),
        name="local_terms",
    )(q, k, v, gt, index, table)


def query_kernel(levels, pieces, head_size, last, pos_ref, *refs):
    refs = list(refs)
    gt_ref, index_ref, table_ref, base_ref = refs[:4]
    del refs[:4]
    arrived = refs[: -3]
    out_ref, weights, total = refs[-3:]
    step = pl.program_id(0)
    pos = pos_ref[0]
    width = gt_ref.shape[0]
    heads = width // head_size

    @pl.when(step == 0)
    def _():
        for i, level in enumerate(levels):
            weights[i] = level_weights(index_ref, table_ref, level)
        total[...] = base_ref[...]

    first = (step ^ (pos & 3)) * heads
    for i, level in enumerate(levels):
        bit = (pos >> (level - 1)) & 1

        @pl.when(bit == 1)
        def _():
            scaled = scaled_rows(
                gt_ref[...], lambda h: weights[i, pl.ds(first + h, 1), :], head_size, heads
            )
            for r in range(PARTS):

                @pl.when(step == r)
                def _():
                    total[...] += dot(pieces(arrived, level, r), scaled)

    @pl.when(step == PARTS - 1)
    def _():
        if last:
            out_ref[...] = total[...].T.astype(BF16)
        else:
            out_ref[...] = total[...]


def query_terms(pos, gt, index, table, base, arrived, levels, pieces, head_size, last):
    state, tokens = base.shape
    columns = gt.shape[0]
    width = columns // PARTS
    whole = lambda s, p: (0, 0)
    shape = (tokens, state) if last else (state, tokens)
    return pl.pallas_call(
        functools.partial(query_kernel, levels, pieces, head_size, last),
        grid_spec=pltpu.PrefetchScalarGridSpec(
            num_scalar_prefetch=1,
            grid=(PARTS,),
            in_specs=[
                pl.BlockSpec((width, tokens), lambda s, p: (s ^ (p[0] & 3), 0)),
                pl.BlockSpec(index.shape, whole),
                pl.BlockSpec(table.shape, lambda s, p: (0, 0, 0)),
                pl.BlockSpec(base.shape, whole),
            ]
            + [whole_spec(a, 2) for a in arrived],
            out_specs=pl.BlockSpec(shape, whole),
            scratch_shapes=[
                pltpu.VMEM((len(levels), table.shape[2], tokens), F32),
                pltpu.VMEM((state, tokens), F32),
            ],
        ),
        out_shape=jax.ShapeDtypeStruct(shape, BF16 if last else F32),
        cost_estimate=pl.CostEstimate(
            flops=4 * tokens * state * columns * len(levels),
            bytes_accessed=2 * tokens * columns,
            transcendentals=0,
        ),
        name="query_terms_" + "_".join(map(str, levels)),
    )(pos, gt, index, table, base, *arrived)


def whole_spec(array, n_args):
    zeros = (0,) * array.ndim
    if n_args == 2:
        return pl.BlockSpec(array.shape, lambda s, p: zeros)
    return pl.BlockSpec(array.shape, lambda s: zeros)


def gather_state(levels, pieces, arrived, pos, state_ref):
    for r in range(PARTS):
        total = jnp.zeros(state_ref.shape[1:], F32)
        for level in levels:
            clear = ((pos >> (level - 1)) & 1) == 0
            piece = pieces(arrived, level, r).astype(F32)
            total = total + jnp.where(clear, piece, 0.0)
        state_ref[r] = total.astype(BF16)


def key_kernel(levels, pieces, pos_ref, v_ref, base_ref, *refs):
    arrived, (out_ref, state, total) = refs[:-3], refs[-3:]
    step = pl.program_id(0)

    @pl.when(step == 0)
    def _():
        gather_state(levels, pieces, arrived, pos_ref[0], state)
        total[...] = base_ref[...]

    total[...] += dot(v_ref[...], state[step], ((1,), (1,)))

    @pl.when(step == PARTS - 1)
    def _():
        out_ref[...] = total[...].astype(BF16)


def key_terms(pos, v, base, arrived, levels, pieces):
    tokens, state = base.shape
    columns = v.shape[1]
    width = columns // PARTS
    whole = lambda s, p: (0, 0)
    return pl.pallas_call(
        functools.partial(key_kernel, levels, pieces),
        grid_spec=pltpu.PrefetchScalarGridSpec(
            num_scalar_prefetch=1,
            grid=(PARTS,),
            in_specs=[
                pl.BlockSpec((tokens, width), lambda s, p: (0, s ^ (p[0] & 3))),
                pl.BlockSpec(base.shape, whole),
            ]
            + [whole_spec(a, 2) for a in arrived],
            out_specs=pl.BlockSpec(base.shape, whole),
            scratch_shapes=[
                pltpu.VMEM((PARTS, state, width), BF16),
                pltpu.VMEM(base.shape, F32),
            ],
        ),
        out_shape=jax.ShapeDtypeStruct(base.shape, BF16),
        cost_estimate=pl.CostEstimate(
            flops=4 * tokens * state * columns,
            bytes_accessed=2 * tokens * columns,
            transcendentals=0,
        ),
        name="key_terms",
    )(pos, v, base, *arrived)


def value_kernel(levels, pieces, head_size, pos_ref, q_ref, k_ref, gt_ref, index_ref, table_ref, *refs):
    arrived, (out_ref, state, masked, weights) = refs[:-4], refs[-4:]
    step = pl.program_id(0)
    pos = pos_ref[0]
    tokens = q_ref.shape[0]
    tile = min(TILE, tokens)
    heads = gt_ref.shape[0] // head_size

    @pl.when(step == 0)
    def _():
        gather_state(levels, pieces, arrived, pos, state)
        weights[...] = level_weights(index_ref, table_ref, 0)
        for i in range(tokens // tile):
            low = i * tile
            scores = dot(k_ref[low : low + tile, :], q_ref[low:, :], ((1,), (1,)))
            s_ids = lax.broadcasted_iota(jnp.int32, scores.shape, 0)
            t_ids = lax.broadcasted_iota(jnp.int32, scores.shape, 1)
            masked[low : low + tile, low:] = jnp.where(s_ids <= t_ids, scores, 0.0).astype(BF16)

    first = (step ^ (pos & 3)) * heads
    scaled = scaled_rows(
        gt_ref[...], lambda h: weights[pl.ds(first + h, 1), :], head_size, heads
    )
    for i in range(tokens // tile):
        low = i * tile
        near = dot(masked[low : low + tile, low:], scaled[:, low:], ((1,), (1,)))
        far = dot(k_ref[low : low + tile, :], state[step])
        out_ref[low : low + tile, :] = (near + far).astype(BF16)


def value_terms(pos, q, k, gt, index, table, arrived, levels, pieces, head_size):
    tokens, state = q.shape
    columns = gt.shape[0]
    width = columns // PARTS
    whole = lambda s, p: (0, 0)
    return pl.pallas_call(
        functools.partial(value_kernel, levels, pieces, head_size),
        grid_spec=pltpu.PrefetchScalarGridSpec(
            num_scalar_prefetch=1,
            grid=(PARTS,),
            in_specs=[
                pl.BlockSpec(q.shape, whole),
                pl.BlockSpec(k.shape, whole),
                pl.BlockSpec((width, tokens), lambda s, p: (s ^ (p[0] & 3), 0)),
                pl.BlockSpec(index.shape, whole),
                pl.BlockSpec(table.shape, lambda s, p: (0, 0, 0)),
            ]
            + [whole_spec(a, 2) for a in arrived],
            out_specs=pl.BlockSpec((tokens, width), lambda s, p: (0, s ^ (p[0] & 3))),
            scratch_shapes=[
                pltpu.VMEM((PARTS, state, width), BF16),
                pltpu.VMEM((tokens, tokens), BF16),
                pltpu.VMEM((table.shape[2], tokens), F32),
            ],
        ),
        out_shape=jax.ShapeDtypeStruct((tokens, columns), BF16),
        cost_estimate=pl.CostEstimate(
            flops=2 * tokens * tokens * columns,
            bytes_accessed=4 * tokens * columns,
            transcendentals=0,
        ),
        name="value_terms",
    )(pos, q, k, gt, index, table, *arrived)


def add(left, right):
    return (left.astype(F32) + right.astype(F32)).astype(BF16)


def low_piece(arrived, level, r):
    one, two_here, two_core = arrived
    if level == 1:
        place = r ^ 1
        return one[1 - place % 2, place >> 1]
    if r % 2 == 0:
        return two_here[(r ^ 2) >> 1]
    return two_core[(r ^ 3) >> 1]


def high_piece(arrived, level, r):
    here, chip, core = arrived
    i = level - 3
    if r == 0:
        return here[i]
    if r == 2:
        return chip[i]
    return core[r >> 1, i]


def any_piece(arrived, level, r):
    if level < 3:
        return low_piece(arrived[:3], level, r)
    return high_piece(arrived[3:], level, r)


def per_device(queries, key_rows, value_rows, out_grad, level_index, level_table):
    columns = value_rows.shape[1]
    head_size = columns // level_table.shape[2]
    depth = lax.axis_size("seq").bit_length() - 1
    pos = lax.axis_index("seq").astype(jnp.int32)[None]
    index = level_index.T
    table = level_table
    low, high = (1, 2), tuple(range(3, depth + 1))

    *halves, gt = slots(
        pos, queries, key_rows, value_rows, out_grad, index, table, high, head_size, True
    )
    send = jnp.stack(halves[0::2], axis=1)
    keep = jnp.stack(halves[1::2], axis=1)
    got = exchange(send, 1)
    leave = add(keep[1], got[1])
    own = add(keep[0], got[0])
    send1, keep1, send2, keep2 = slots(
        pos, queries, key_rows, value_rows, gt, index, table, low, head_size, False
    )
    own = add(own, exchange(leave, 2))
    one = exchange(jnp.stack([send1, keep1]), 1)
    half2 = add(keep2, exchange(send2, 1))
    two_here = exchange(half2, 2)
    two_core = exchange(two_here, 1)
    query_local, key_local = local_terms(
        queries, key_rows, value_rows, gt, index, table, head_size
    )
    here = []
    for j in range(2, depth):
        got = exchange(own, (1 << (j + 1)) - 4)
        here.append(got[0])
        own = add(own[1:], got[1:])
    here = jnp.stack(here)
    low_arrived = (one, two_here, two_core)
    query_low = query_terms(
        pos, gt, index, table, query_local, low_arrived, low, low_piece, head_size, False
    )
    chip = exchange(here, 2)
    core = exchange(jnp.stack([here, chip]), 1)
    high_arrived = (here, chip, core)
    arrived = low_arrived + high_arrived
    key_part = key_terms(pos, value_rows, key_local, arrived, low + high, any_piece)
    query_part = query_terms(
        pos, gt, index, table, query_low, high_arrived, high, high_piece, head_size, True
    )
    key_grad = head_sum(key_part)
    query_grad = head_sum(query_part)
    value_grad = value_terms(
        pos, queries, key_rows, gt, index, table, arrived, low + high, any_piece, head_size
    )
    return query_grad, key_grad, value_grad


def solution(mesh):
    return jax.shard_map(
        per_device,
        mesh=mesh,
        in_specs=(
            P("seq", None),
            P("seq", None),
            P("seq", "head"),
            P("seq", "head"),
            P("seq", None),
            P(None, None, "head"),
        ),
        out_specs=(P("seq", None), P("seq", None), P("seq", "head")),
        check_vma=False,
    )
```
